512 devices in a mesh: grp: 64 (over y, z), sta: 8 (over x, core).
Axes of the slice: x: 4, y: 8, z: 8, core: 2. Of those that a mesh axis runs over, the one named last changes fastest.
Arguments:
- seismograms: float32 [2048, 16, 4, 2063], P(('grp', 'sta')), may hold values from -6 to 6
- fir_taps: float32 [4, 16], replicated, may hold values from -0.75 to 0.75
- valid_windows: int32 [2048, 16], P('grp'), may hold values from 0 to 1, as said below
- pair_owners: int32 [64, 72, 1], P('grp'), may hold values from 0 to 63; in each aligned block of 72 rows (0 to 71, 72 to 143, ..., all dimensions but the last counted through in order) at most 2 rows name the same one
Outputs:
- correlations: float32 [64, 64, 2, 8, 2001], P('grp', None, None, 'sta')
The draws below stay inside these ranges and needn't reach their ends.
Inputs may be any that keep to these rules, and one draw needn't show every extreme that they name: `pair_owners`: among the 72 pair blocks of one group, at most 2 have the same owner. `valid_windows`: some stations, at least one, have no usable window at all.
All inputs are finite; a program needn't handle non-finite values.
Results may differ from the reference program's by a relative error of at most 0.0027.
Values may be sent and summed in bfloat16 or wider, within the bound.
A program may use at most 64 MiB of HBM per device.

```python
import math
import jax
import jax.numpy as jnp
import numpy as np
from jax import lax

ST = 4
WIN = 16
SEG = 2048
TAPQ = 16
NB = 256
K0 = 16
SMOOTH = 32
MAXLAG = 1000
CAP = 2
SPLIT = 2
STATIONS = 2048
SB = 2
PBG = 72
SEGP = 2063
N_GRP = 64
N_STA = 8


def draw_valid_windows(key, part):
    usable_key = jax.random.fold_in(key, 11)
    roll_key = jax.random.fold_in(key, 12)
    chosen_key = jax.random.fold_in(key, 13)
    usable = (jax.random.randint(usable_key, (STATIONS, WIN), 0, 4) < 3).astype(jnp.int32)
    station_roll = jax.random.randint(roll_key, (STATIONS,), 0, 32)
    chosen = jax.random.randint(chosen_key, (), 0, STATIONS)
    silent = (station_roll == 0) | (jnp.arange(STATIONS, dtype=jnp.int32) == chosen)
    return jnp.where(silent[:, None], 0, usable).astype(jnp.int32)


def steps_of(stream_key, shape, shards, smallest, largest):
    def one(axis_at, blocks):
        draws = jax.random.uniform(jax.random.fold_in(jax.random.fold_in(stream_key, 6), axis_at), (blocks,), jnp.float32, smallest / len(shards), largest / len(shards))
        return jnp.repeat(jnp.exp(draws), shape[axis_at] // blocks).reshape((-1,) + (1,) * (len(shape) - axis_at - 1))

    level = one(*shards[0])
    for cut in shards[1:]:
        level = level * one(*cut)
    return level


def routed_block(stream_key, own, number, rows, count, top, limit, slope):
    sequence = jax.random.permutation(stream_key, count)
    heavy_load, ordinary = load_shares(count, rows * top, limit, slope, True), load_shares(count, rows * top, limit, slope, False)
    places = jnp.arange(count)

    def named(lengths, offset_by):
        used = int((lengths > 0).sum())
        fixed = max(1, used // 4)
        moved = fixed + (places - fixed + offset_by * (used - fixed)) % max(1, count - fixed)
        return jnp.zeros((count,), jnp.int32).at[sequence[jnp.where(places < fixed, places, moved)]].set(jnp.asarray(lengths, jnp.int32))

    lengths = jnp.where(number % 4 == 0, named(heavy_load, number // 4), named(ordinary, number - number // 4 - 1))
    mixed = jax.random.permutation(jax.random.fold_in(own, 3), count)
    donor, taker = mixed[0:count // 2 * 2:2], mixed[1:count // 2 * 2:2]
    slack = jnp.minimum(lengths[donor] - 1, limit - lengths[taker]) // 2
    slack = jnp.where((donor == sequence[0]) | (taker == sequence[0]) | (lengths[taker] == 0), 0, jnp.maximum(slack, 0))
    moved = jax.random.randint(jax.random.fold_in(own, 4), (count // 2,), 0, 1 << 20) % (slack + 1)
    lengths = lengths.at[donor].add(-moved).at[taker].add(moved)
    labels = jnp.searchsorted(jnp.cumsum(lengths), jnp.arange(rows * top), side="right").astype(jnp.int32)
    table = labels.reshape(top, rows).T
    table = table[jax.random.permutation(jax.random.fold_in(own, 1), rows)]
    offset_by = jax.random.randint(jax.random.fold_in(own, 2), (rows, 1), 0, top)
    return jnp.take_along_axis(table, (jnp.arange(top)[None, :] + offset_by) % top, axis=1)


def load_shares(count, total, bound, lean, full):
    weights = [(1 << 20) // math.isqrt(grade ** lean) + 1 for grade in range(1, count + 1)]
    largest = bound if full else min(bound, max(-(-total // count), total * weights[0] // sum(weights)))
    least = 1 if total - largest >= count - 1 else 0
    counts, spare = [largest] + [least] * (count - 1), total - largest - least * (count - 1)
    while spare > 0:
        movable = [i for i in range(1, count) if counts[i] < largest] or [i for i in range(1, count) if counts[i] < bound]
        whole, remaining = sum([weights[i] for i in movable]), spare
        for i in movable:
            more = min(bound - counts[i], max(1, remaining * weights[i] // whole), spare)
            counts[i] = counts[i] + more
            spare = spare - more
    return np.array(counts)


def bell_draw(stream_key, extent, scale, limit, shards=(), held_as=jnp.bfloat16):
    level = steps_of(stream_key, extent, shards, -0.22, 0.18) if shards else 1.0
    drawn = jax.random.normal(stream_key, extent, jnp.float32) * scale * level
    return jnp.minimum(jnp.maximum(drawn, -limit), limit).astype(held_as)


def setup_inputs(seed: int = 0) -> dict:
    seeds = jax.random.split(jax.random.key(seed), 5)
    seismograms = bell_draw(seeds[0], (STATIONS, WIN, 4, SEGP), 1.0, 6.0, ((0, 512),), jnp.float32)
    fir_taps = bell_draw(seeds[1], (4, TAPQ), (4 * TAPQ) ** -0.5, 0.75, (), jnp.float32)
    valid_windows = draw_valid_windows(jax.random.fold_in(seeds[4], 71), 0)
    pair_owners_keys = jax.random.split(jax.random.fold_in(seeds[3], 1), N_GRP * PBG // PBG)
    pair_owners_turns = jax.random.permutation(jax.random.fold_in(seeds[3], 3), N_GRP * PBG // PBG)
    pair_owners = jax.vmap(lambda own, number: routed_block(jax.random.fold_in(seeds[3], 2), own, number, PBG, N_GRP, 1, CAP, 2))(pair_owners_keys, pair_owners_turns).reshape((N_GRP, PBG, 1))
    return dict(seismograms=seismograms, fir_taps=fir_taps, valid_windows=valid_windows, pair_owners=pair_owners)


EPSILON = 1e-06

def decimate(raw_block, fir_taps):
    samples = raw_block.shape[-1] - fir_taps.shape[1] + 1
    filtered = jnp.zeros(raw_block.shape[:2] + (samples,), jnp.float32)
    for offset in range(fir_taps.shape[1]):
        segment_part = raw_block[:, :, :, offset:offset + samples]
        filtered = filtered + lax.optimization_barrier(jnp.sum(segment_part * fir_taps[None, None, :, offset:offset + 1], axis=2))
    return filtered

def smoother():
    positions = jnp.arange(NB)
    nearby = jnp.abs(positions[:, None] - positions[None, :]) <= SMOOTH
    return nearby.astype(jnp.float32) / (2 * SMOOTH + 1)

def one_group(operands, fir_taps):
    raw_group, valid_group, owners_group = operands
    series = decimate(raw_group, fir_taps)
    spectrum = jnp.fft.rfft(series, n=2 * SEG, axis=-1)[..., K0:K0 + NB]
    real_part = jnp.real(spectrum).astype(jnp.float32)
    imag_part = jnp.imag(spectrum).astype(jnp.float32)
    band_power = real_part * real_part + imag_part * imag_part
    smoothed = jnp.einsum('swk,kj->swj', band_power, smoother(), precision=lax.Precision.HIGHEST)
    whitener = valid_group.astype(jnp.float32)[..., None] / jnp.sqrt(smoothed + EPSILON)
    white_re = lax.optimization_barrier((real_part * whitener).astype(jnp.bfloat16)).astype(jnp.float32)
    white_im = lax.optimization_barrier((imag_part * whitener).astype(jnp.bfloat16)).astype(jnp.float32)
    row_blocks, col_blocks = np.triu_indices(N_STA)
    block_count = row_blocks.shape[0]
    pair_total = block_count * SPLIT
    blocks_re = white_re.reshape(N_STA, ST, WIN, NB)
    blocks_im = white_im.reshape(N_STA, ST, WIN, NB)
    left_re, right_re = (blocks_re[row_blocks], blocks_re[col_blocks])
    left_im, right_im = (blocks_im[row_blocks], blocks_im[col_blocks])
    high = lax.Precision.HIGHEST
    stack_re = jnp.einsum('pawk,pbwk->pabk', left_re, right_re, precision=high) + jnp.einsum('pawk,pbwk->pabk', left_im, right_im, precision=high)
    stack_im = jnp.einsum('pawk,pbwk->pabk', left_im, right_re, precision=high) - jnp.einsum('pawk,pbwk->pabk', left_re, right_im, precision=high)
    valid_blocks = valid_group.astype(jnp.float32).reshape(N_STA, ST, WIN)
    pair_count = jnp.einsum('paw,pbw->pab', valid_blocks[row_blocks], valid_blocks[col_blocks], precision=high).reshape(pair_total, SB * ST)
    widths = ((0, 0), (0, 0), (K0, SEG + 1 - K0 - NB))
    padded_re = jnp.pad(stack_re.reshape(pair_total, SB * ST, NB), widths)
    padded_im = jnp.pad(stack_im.reshape(pair_total, SB * ST, NB), widths)
    circular = jnp.fft.irfft(lax.complex(padded_re, padded_im), n=2 * SEG, axis=-1) * SEG
    lag_ids = (jnp.arange(2 * MAXLAG + 1, dtype=jnp.int32) - MAXLAG) % (2 * SEG)
    normalizer = 1.0 / (math.sqrt(NB) * jnp.maximum(pair_count, 1.0))
    lagged = circular[..., lag_ids] * normalizer[..., None]
    owner_ids = owners_group[:, 0]
    pair_ids = jnp.arange(pair_total, dtype=jnp.int32)
    earlier = pair_ids[None, :] < pair_ids[:, None]
    same_owner = owner_ids[:, None] == owner_ids[None, :]
    slot_index = lax.optimization_barrier(jnp.sum((earlier & same_owner).astype(jnp.int32), axis=1))
    placed = jnp.zeros((N_GRP, CAP, SB * ST, 2 * MAXLAG + 1), jnp.float32)
    return placed.at[owner_ids, slot_index].set(lagged)

def reference(seismograms, fir_taps, valid_windows, pair_owners):
    raw_groups = seismograms.reshape((N_GRP, -1) + seismograms.shape[1:])
    valid_groups = valid_windows.reshape(N_GRP, -1, valid_windows.shape[1])
    by_source = lax.map(lambda operands: one_group(operands, fir_taps), (raw_groups, valid_groups, pair_owners))
    return jnp.transpose(by_source, (1, 0, 2, 3, 4))
```

```python
import math

import jax
import jax.numpy as jnp
import numpy as np
from jax import lax
from jax.sharding import PartitionSpec as P

SEG = 2048
NB = 256
K0 = 16
SMOOTH = 32
MAXLAG = 1000
CAP = 2
SPLIT = 2
STEP = 64

EPSILON = 1e-06
PRECISE = lax.Precision.HIGHEST
FREQS = K0 + np.arange(NB)


def turn(multiples):
    angle = (np.asarray(multiples)[:, None] * FREQS[None, :] % (2 * SEG)) * (math.pi / SEG)
    return np.cos(angle).astype(np.float32), (-np.sin(angle)).astype(np.float32)


def wave_table():
    coarse_re, coarse_im = turn(STEP * np.arange(SEG // STEP))
    fine_re, fine_im = turn(np.arange(STEP))
    cr, ci = coarse_re[:, None], coarse_im[:, None]
    fr, fi = fine_re[None], fine_im[None]
    real = jnp.asarray(cr) * fr - jnp.asarray(ci) * fi
    imag = jnp.asarray(cr) * fi + jnp.asarray(ci) * fr
    return jnp.concatenate([real.reshape(SEG, NB), imag.reshape(SEG, NB)], axis=1)


def smoother():
    near = np.abs(np.arange(NB)[:, None] - np.arange(NB)[None, :]) <= SMOOTH
    return near.astype(np.float32) / (2 * SMOOTH + 1)


def spectra_of(seismograms, fir_taps, table):
    stations, windows, phases, _ = seismograms.shape
    taps = fir_taps.shape[1]
    rows = stations * windows
    raw = seismograms.reshape(rows, phases, -1)
    main = raw[:, :, :SEG].reshape(rows * phases, SEG)
    whole = jnp.dot(main, table, precision=lax.Precision.HIGH, preferred_element_type=jnp.float32)
    whole = whole.reshape(rows, phases, 2 * NB)
    whole_re, whole_im = whole[..., :NB], whole[..., NB:]
    adv_re, adv_im = turn(-np.arange(taps))
    gain_re = jnp.dot(fir_taps, adv_re, precision=PRECISE)
    gain_im = jnp.dot(fir_taps, adv_im, precision=PRECISE)
    real = jnp.sum(whole_re * gain_re - whole_im * gain_im, axis=1)
    imag = jnp.sum(whole_re * gain_im + whole_im * gain_re, axis=1)
    padded = jnp.pad(fir_taps, ((0, 0), (0, taps)))
    shifted = jnp.stack([padded[:, j : j + taps - 1] for j in range(1, taps)], axis=-1)
    shifted = shifted.reshape(phases * (taps - 1), taps - 1)
    head = jnp.dot(raw[:, :, : taps - 1].reshape(rows, -1), shifted, precision=PRECISE)
    tail = jnp.dot(raw[:, :, SEG:].reshape(rows, -1), shifted, precision=PRECISE)
    sign = np.where(FREQS % 2 == 0, 1.0, -1.0).astype(np.float32)
    edge = np.concatenate([adv_re[1:], adv_im[1:]], axis=1)
    edges = np.concatenate([-edge, edge * np.concatenate([sign, sign])], axis=0)
    fix = jnp.dot(jnp.concatenate([head, tail], axis=1), edges, precision=PRECISE)
    return real + fix[:, :NB], imag + fix[:, NB:]


def local(seismograms, fir_taps, valid_windows, pair_owners):
    stations, windows = seismograms.shape[:2]
    members = lax.axis_size("sta")
    groups = lax.axis_size("grp")
    member = lax.axis_index("sta")
    table = wave_table()
    real, imag = spectra_of(seismograms, fir_taps, table)
    own_valid = lax.dynamic_slice_in_dim(valid_windows, member * stations, stations, 0)
    smoothed = jnp.dot(real * real + imag * imag, smoother(), precision=PRECISE)
    whitener = own_valid.reshape(-1, 1).astype(jnp.float32) / jnp.sqrt(smoothed + EPSILON)
    white = jnp.concatenate([real * whitener, imag * whitener], axis=1).astype(jnp.bfloat16)
    white = white.reshape(stations, windows, 2 * NB)
    gathered = lax.all_gather(white, "sta", axis=0, tiled=False)

    side_a, side_c = member // stations, member % stations
    left_rows = stations // SPLIT
    left = gathered.reshape(members, SPLIT, left_rows, windows, 2 * NB)
    left = lax.dynamic_index_in_dim(left, side_a, 2, keepdims=False).astype(jnp.float32)
    right = lax.dynamic_index_in_dim(gathered, side_c, 1, keepdims=False).astype(jnp.float32)
    lr, li = left[:, :, None, :, :NB], left[:, :, None, :, NB:]
    rr, ri = right[None, None, :, :, :NB], right[None, None, :, :, NB:]
    stack_re = jnp.sum(lr * rr + li * ri, axis=3)
    stack_im = jnp.sum(li * rr - lr * ri, axis=3)
    mask = valid_windows.astype(jnp.float32)
    mask_left = mask.reshape(members, SPLIT, left_rows, windows)
    mask_left = lax.dynamic_index_in_dim(mask_left, side_a, 2, keepdims=False)
    mask_right = mask.reshape(members, stations, windows)
    mask_right = lax.dynamic_index_in_dim(mask_right, side_c, 1, keepdims=False)
    count = jnp.einsum("ihw,jw->ihj", mask_left, mask_right, precision=PRECISE)
    scale = (1.0 / (math.sqrt(NB) * jnp.maximum(count, 1.0)))[..., None]
    lead_re, lead_im = turn([MAXLAG])
    moved_re = (stack_re * lead_re - stack_im * lead_im) * scale
    moved_im = (stack_re * lead_im + stack_im * lead_re) * scale
    combos = members * SPLIT * members
    moved = jnp.concatenate([moved_re, moved_im], axis=-1).reshape(combos, 2 * NB)
    moved = moved.astype(jnp.bfloat16)

    rows_of, cols_of = np.triu_indices(members)
    pair_i = np.repeat(rows_of, SPLIT)
    pair_j = np.repeat(cols_of, SPLIT)
    pair_h = np.tile(np.arange(SPLIT), rows_of.shape[0])
    combo_of = (pair_i * SPLIT + pair_h) * members + pair_j
    owners = pair_owners[0, :, 0]
    blocks = owners.shape[0]
    earlier = np.arange(blocks)[None, :] < np.arange(blocks)[:, None]
    slot = jnp.sum((earlier & (owners[:, None] == owners[None, :])).astype(jnp.int32), axis=1)
    place = owners * CAP + slot
    spread = np.zeros((blocks, combos), np.float32)
    spread[np.arange(blocks), combo_of] = 1.0
    onto = (place[None, :] == jnp.arange(groups * CAP, dtype=jnp.int32)[:, None])
    onto = jnp.dot(onto.astype(jnp.bfloat16), jnp.asarray(spread, jnp.bfloat16), preferred_element_type=jnp.float32)
    routed = jnp.dot(onto.astype(jnp.bfloat16), moved, preferred_element_type=jnp.float32)
    routed = routed.astype(jnp.bfloat16).reshape(groups, CAP, 2 * NB)
    arrived = lax.all_to_all(routed, "grp", split_axis=0, concat_axis=0, tiled=True)
    waves = table.astype(jnp.bfloat16)[: 2 * MAXLAG + 1]
    lagged = lax.dot_general(
        arrived.reshape(groups * CAP, 2 * NB),
        waves,
        (((1,), (1,)), ((), ())),
        preferred_element_type=jnp.float32,
    )
    return lagged.reshape(1, groups, CAP, 1, 2 * MAXLAG + 1)


def solution(mesh):
    in_specs = (P(("grp", "sta"), None, None, None), P(), P("grp", None), P("grp", None, None))
    out_specs = P("grp", None, None, "sta", None)
    return jax.shard_map(local, mesh=mesh, in_specs=in_specs, out_specs=out_specs, check_vma=False)
```

```python
import functools
import math

import jax
import jax.numpy as jnp
import numpy as np
from jax import lax
from jax.experimental import pallas as pl
from jax.experimental.pallas import tpu as pltpu
from jax.sharding import PartitionSpec as P

SEG = 2048
NB = 256
K0 = 16
SMOOTH = 32
MAXLAG = 1000
CAP = 2
SPLIT = 2
STEP = 64

EPSILON = 1e-06
PRECISE = lax.Precision.HIGHEST
FREQS = K0 + np.arange(NB)


def turn(multiples):
    angle = (np.asarray(multiples)[:, None] * FREQS[None, :] % (2 * SEG)) * (math.pi / SEG)
    return np.cos(angle).astype(np.float32), (-np.sin(angle)).astype(np.float32)


def wave_table():
    coarse_re, coarse_im = turn(STEP * np.arange(SEG // STEP))
    fine_re, fine_im = turn(np.arange(STEP))
    cr, ci = coarse_re[:, None], coarse_im[:, None]
    fr, fi = fine_re[None], fine_im[None]
    real = jnp.asarray(cr) * fr - jnp.asarray(ci) * fi
    imag = jnp.asarray(cr) * fi + jnp.asarray(ci) * fr
    return jnp.concatenate([real.reshape(SEG, NB), imag.reshape(SEG, NB)], axis=1)


def smoother():
    near = np.abs(np.arange(NB)[:, None] - np.arange(NB)[None, :]) <= SMOOTH
    return near.astype(np.float32) / (2 * SMOOTH + 1)


def spectra_of(seismograms, fir_taps, table):
    stations, windows, phases, _ = seismograms.shape
    taps = fir_taps.shape[1]
    rows = stations * windows
    raw = seismograms.reshape(rows, phases, -1)
    main = raw[:, :, :SEG].reshape(rows * phases, SEG)
    whole = jnp.dot(main, table, precision=lax.Precision.HIGH, preferred_element_type=jnp.float32)
    whole = whole.reshape(rows, phases, 2 * NB)
    whole_re, whole_im = whole[..., :NB], whole[..., NB:]
    adv_re, adv_im = turn(-np.arange(taps))
    gain_re = jnp.dot(fir_taps, adv_re, precision=PRECISE)
    gain_im = jnp.dot(fir_taps, adv_im, precision=PRECISE)
    real = jnp.sum(whole_re * gain_re - whole_im * gain_im, axis=1)
    imag = jnp.sum(whole_re * gain_im + whole_im * gain_re, axis=1)
    padded = jnp.pad(fir_taps, ((0, 0), (0, taps)))
    shifted = jnp.stack([padded[:, j : j + taps - 1] for j in range(1, taps)], axis=-1)
    shifted = shifted.reshape(phases * (taps - 1), taps - 1)
    head = jnp.dot(raw[:, :, : taps - 1].reshape(rows, -1), shifted, precision=PRECISE)
    tail = jnp.dot(raw[:, :, SEG:].reshape(rows, -1), shifted, precision=PRECISE)
    sign = np.where(FREQS % 2 == 0, 1.0, -1.0).astype(np.float32)
    edge = np.concatenate([adv_re[1:], adv_im[1:]], axis=1)
    edges = np.concatenate([-edge, edge * np.concatenate([sign, sign])], axis=0)
    fix = jnp.dot(jnp.concatenate([head, tail], axis=1), edges, precision=PRECISE)
    return real + fix[:, :NB], imag + fix[:, NB:]


def combine(members, groups, stations, windows, *refs):
    (spec_ref, valid_ref, smooth_ref, lead_ref, scale_ref, onto_ref, out_ref) = refs[:7]
    white, left, right, stack, staged, routed, arrived = refs[7:14]
    near_send, near_recv, far_send, far_recv = refs[14:]
    mine = lax.axis_index("sta")
    group = lax.axis_index("grp")
    half = stations // SPLIT

    barrier = pltpu.get_barrier_semaphore()

    @pl.loop(1, groups)
    def _(k):
        pl.semaphore_signal(
            barrier,
            inc=1,
            device_id={"grp": lax.rem(group + k, groups)},
            device_id_type=pl.DeviceIdType.MESH,
        )

    @pl.loop(1, members)
    def _(k):
        pl.semaphore_signal(
            barrier,
            inc=1,
            device_id={"sta": lax.rem(mine + k, members)},
            device_id_type=pl.DeviceIdType.MESH,
        )

    real, imag = spec_ref[:, :NB], spec_ref[:, NB:]
    smoothed = jnp.dot(
        real * real + imag * imag,
        smooth_ref[...],
        precision=PRECISE,
        preferred_element_type=jnp.float32,
    )
    whitener = valid_ref[...] / jnp.sqrt(smoothed + EPSILON)
    white[:, :, :NB] = (real * whitener).astype(jnp.bfloat16).reshape(stations, windows, NB)
    white[:, :, NB:] = (imag * whitener).astype(jnp.bfloat16).reshape(stations, windows, NB)

    def near(k):
        peer = lax.rem(mine + k, members)
        side_a, side_c = peer // stations, lax.rem(peer, stations)
        copies = []
        for part in range(SPLIT + 1):
            station = side_c if part == SPLIT else part * half + side_a
            into = right.at[mine] if part == SPLIT else left.at[mine, part]
            copies.append(
                pltpu.make_async_remote_copy(
                    src_ref=white.at[station],
                    dst_ref=into,
                    send_sem=near_send.at[k, part],
                    recv_sem=near_recv.at[k, part],
                    device_id={"sta": peer},
                    device_id_type=pl.DeviceIdType.MESH,
                )
            )
        return copies

    pl.semaphore_wait(barrier, members - 1 + groups - 1)
    for k in range(1, members):
        for copy in near(k):
            copy.start()
    for part in range(SPLIT):
        left[mine, part] = white[part * half + mine // stations]
    right[mine] = white[lax.rem(mine, stations)]
    for k in range(1, members):
        for copy in near(k):
            copy.wait()

    @pl.loop(0, members * SPLIT)
    def _(n):
        i, h = n // SPLIT, lax.rem(n, SPLIT)
        ours = left[i, h].astype(jnp.float32)
        theirs = right[...].astype(jnp.float32)
        lr, li = ours[None, :, :NB], ours[None, :, NB:]
        rr, ri = theirs[:, :, :NB], theirs[:, :, NB:]
        rows = pl.ds(pl.multiple_of(n * members, members), members)
        stack[rows, :NB] = jnp.sum(lr * rr + li * ri, axis=1)
        stack[rows, NB:] = jnp.sum(li * rr - lr * ri, axis=1)

    lead_re, lead_im = lead_ref[0:1], lead_ref[1:2]
    stack_re, stack_im = stack[:, :NB], stack[:, NB:]
    moved_re = ((stack_re * lead_re - stack_im * lead_im) * scale_ref[...]).astype(jnp.bfloat16)
    moved_im = ((stack_re * lead_im + stack_im * lead_re) * scale_ref[...]).astype(jnp.bfloat16)
    for slot in range(CAP):
        for part, moved in enumerate((moved_re, moved_im)):
            placed = jnp.dot(onto_ref[slot], moved, preferred_element_type=jnp.float32)
            for chunk in range(NB // 128):
                row = slot * (2 * NB // 128) + part * (NB // 128) + chunk
                staged[:, row, :] = placed[:, chunk * 128 : (chunk + 1) * 128]
    routed[...] = staged[...].astype(jnp.bfloat16)

    def far(k):
        peer = lax.rem(group + k, groups)
        return pltpu.make_async_remote_copy(
            src_ref=routed.at[peer],
            dst_ref=arrived.at[group],
            send_sem=far_send.at[k],
            recv_sem=far_recv.at[k],
            device_id={"grp": peer},
            device_id_type=pl.DeviceIdType.MESH,
        )

    @pl.loop(1, groups)
    def _(k):
        far(k).start()

    arrived[group] = routed[group]

    @pl.loop(1, groups)
    def _(k):
        far(k).wait()

    out_ref[...] = arrived[...]


def local(seismograms, fir_taps, valid_windows, pair_owners):
    stations, windows = seismograms.shape[:2]
    members = lax.axis_size("sta")
    groups = lax.axis_size("grp")
    member = lax.axis_index("sta")
    table = wave_table()
    real, imag = spectra_of(seismograms, fir_taps, table)
    own_valid = lax.dynamic_slice_in_dim(valid_windows, member * stations, stations, 0)
    own_valid = own_valid.reshape(-1, 1).astype(jnp.float32)

    side_a, side_c = member // stations, member % stations
    left_rows = stations // SPLIT
    mask = valid_windows.astype(jnp.float32)
    mask_left = mask.reshape(members, SPLIT, left_rows, windows)
    mask_left = lax.dynamic_index_in_dim(mask_left, side_a, 2, keepdims=False)
    mask_right = mask.reshape(members, stations, windows)
    mask_right = lax.dynamic_index_in_dim(mask_right, side_c, 1, keepdims=False)
    combos = members * SPLIT * members
    count = jnp.einsum("ihw,jw->ihj", mask_left, mask_right, precision=PRECISE)
    scale = (1.0 / (math.sqrt(NB) * jnp.maximum(count, 1.0))).reshape(combos, 1)
    lead = jnp.asarray(np.concatenate(turn([MAXLAG])))

    rows_of, cols_of = np.triu_indices(members)
    pair_i = np.repeat(rows_of, SPLIT)
    pair_j = np.repeat(cols_of, SPLIT)
    pair_h = np.tile(np.arange(SPLIT), rows_of.shape[0])
    combo_of = (pair_i * SPLIT + pair_h) * members + pair_j
    owners = pair_owners[0, :, 0]
    blocks = owners.shape[0]
    earlier = np.arange(blocks)[None, :] < np.arange(blocks)[:, None]
    slot = jnp.sum((earlier & (owners[:, None] == owners[None, :])).astype(jnp.int32), axis=1)
    place = slot * groups + owners
    spread = np.zeros((blocks, combos), np.float32)
    spread[np.arange(blocks), combo_of] = 1.0
    onto = (place[None, :] == jnp.arange(groups * CAP, dtype=jnp.int32)[:, None])
    onto = jnp.dot(onto.astype(jnp.bfloat16), jnp.asarray(spread, jnp.bfloat16), preferred_element_type=jnp.float32)
    onto = onto.astype(jnp.bfloat16).reshape(CAP, groups, combos)

    vmem = pl.BlockSpec(memory_space=pltpu.VMEM)
    tile = (groups, CAP * 2 * NB // 128, 128)
    arrived = pl.pallas_call(
        functools.partial(combine, members, groups, stations, windows),
        out_shape=jax.ShapeDtypeStruct(tile, jnp.bfloat16),
        in_specs=[vmem] * 6,
        out_specs=vmem,
        scratch_shapes=[
            pltpu.VMEM((stations, windows, 2 * NB), jnp.bfloat16),
            pltpu.VMEM((members, SPLIT, windows, 2 * NB), jnp.bfloat16),
            pltpu.VMEM((members, windows, 2 * NB), jnp.bfloat16),
            pltpu.VMEM((combos, 2 * NB), jnp.float32),
            pltpu.VMEM(tile, jnp.float32),
            pltpu.VMEM(tile, jnp.bfloat16),
            pltpu.VMEM(tile, jnp.bfloat16),
            pltpu.SemaphoreType.DMA((members, SPLIT + 1)),
            pltpu.SemaphoreType.DMA((members, SPLIT + 1)),
            pltpu.SemaphoreType.DMA((groups,)),
            pltpu.SemaphoreType.DMA((groups,)),
        ],
        compiler_params=pltpu.CompilerParams(collective_id=0, has_side_effects=True),
        name="combine",
    )(jnp.concatenate([real, imag], axis=1), own_valid, jnp.asarray(smoother()), lead, scale, onto)
    waves = table.astype(jnp.bfloat16)[: 2 * MAXLAG + 1]
    lagged = lax.dot_general(
        arrived.reshape(groups * CAP, 2 * NB),
        waves,
        (((1,), (1,)), ((), ())),
        preferred_element_type=jnp.float32,
    )
    return lagged.reshape(1, groups, CAP, 1, 2 * MAXLAG + 1)


def solution(mesh):
    in_specs = (P(("grp", "sta"), None, None, None), P(), P("grp", None), P("grp", None, None))
    out_specs = P("grp", None, None, "sta", None)
    return jax.shard_map(local, mesh=mesh, in_specs=in_specs, out_specs=out_specs, check_vma=False)
```

```python
import functools
import math

import jax
import jax.numpy as jnp
import numpy as np
from jax import lax
from jax.experimental import pallas as pl
from jax.experimental.pallas import tpu as pltpu
from jax.sharding import PartitionSpec as P

SEG = 2048
NB = 256
K0 = 16
SMOOTH = 32
MAXLAG = 1000
CAP = 2
SPLIT = 2
STEP = 64

EPSILON = 1e-06
PRECISE = lax.Precision.HIGHEST
FREQS = K0 + np.arange(NB)


def turn(multiples):
    angle = (np.asarray(multiples)[:, None] * FREQS[None, :] % (2 * SEG)) * (math.pi / SEG)
    return np.cos(angle).astype(np.float32), (-np.sin(angle)).astype(np.float32)


def wave_steps():
    coarse = np.concatenate(turn(STEP * np.arange(SEG // STEP)), axis=1)
    fine = np.concatenate(turn(np.arange(STEP)), axis=1)
    return coarse, fine


def smoother():
    near = np.abs(np.arange(NB)[:, None] - np.arange(NB)[None, :]) <= SMOOTH
    return near.astype(np.float32) / (2 * SMOOTH + 1)


def edge_waves(taps):
    adv = np.concatenate(turn(-np.arange(taps)), axis=1)
    sign = np.where(FREQS % 2 == 0, 1.0, -1.0).astype(np.float32)
    edges = np.zeros((128, 2 * NB), np.float32)
    for j in range(1, taps):
        edges[128 - j] = -adv[j]
        edges[64 - j] = adv[j] * np.concatenate([sign, sign])
    return adv, edges


def pair_spread(members):
    rows_of, cols_of = np.triu_indices(members)
    pair_i = np.repeat(rows_of, SPLIT)
    pair_j = np.repeat(cols_of, SPLIT)
    pair_h = np.tile(np.arange(SPLIT), rows_of.shape[0])
    combo_of = (pair_i * SPLIT + pair_h) * members + pair_j
    spread = np.zeros((combo_of.size, members * SPLIT * members), np.float32)
    spread[np.arange(combo_of.size), combo_of] = 1.0
    return spread


def ints(shape, axis):
    return lax.broadcasted_iota(jnp.int32, shape, axis)


def exact_dot(a, b):
    return jnp.dot(a, b, precision=PRECISE, preferred_element_type=jnp.float32)


def combine(members, groups, stations, windows, phases, *refs):
    (raw_hbm, ends_ref, taps_ref, valid_ref, owners_ref) = refs[:5]
    (coarse_ref, fine_ref, adv_ref, edge_ref, smooth_ref, lead_ref, spread_ref) = refs[5:12]
    out_ref, waves = refs[12:14]
    (raw, rest, whole, white, left, right, stack, held, staged, routed, arrived) = refs[14:25]
    raw_sem, near_send, near_recv, far_send, far_recv = refs[25:]
    mine = lax.axis_index("sta")
    group = lax.axis_index("grp")
    half = stations // SPLIT
    rows = stations * windows

    load = pltpu.make_async_copy(raw_hbm, raw, raw_sem)
    load.start()
    barrier = pltpu.get_barrier_semaphore()

    @pl.loop(1, groups)
    def _(k):
        pl.semaphore_signal(
            barrier,
            inc=1,
            device_id={"grp": lax.rem(group + k, groups)},
            device_id_type=pl.DeviceIdType.MESH,
        )

    @pl.loop(1, members)
    def _(k):
        pl.semaphore_signal(
            barrier,
            inc=1,
            device_id={"sta": lax.rem(mine + k, members)},
            device_id_type=pl.DeviceIdType.MESH,
        )

    @pl.loop(0, SEG // STEP)
    def _(step):
        at = pl.ds(pl.multiple_of(step * STEP, STEP), STEP)
        cr, ci = coarse_ref[pl.ds(step, 1), :NB], coarse_ref[pl.ds(step, 1), NB:]
        fr, fi = fine_ref[:, :NB], fine_ref[:, NB:]
        for part, wave in enumerate((cr * fr - ci * fi, cr * fi + ci * fr)):
            upper = wave.astype(jnp.bfloat16)
            waves[at, part * NB : (part + 1) * NB] = upper
            lower = (wave - upper.astype(jnp.float32)).astype(jnp.bfloat16)
            rest[at, part * NB : (part + 1) * NB] = lower

    phase_taps = taps_ref[...]
    gains = exact_dot(phase_taps, adv_ref[...])
    ends = ends_ref[...]
    past = ends * phase_taps[:, 0:1]
    for q in range(1, phase_taps.shape[1]):
        past = past + pltpu.roll(ends, 128 - q, 1) * phase_taps[:, q : q + 1]
    fix = exact_dot(past, edge_ref[...])
    valid = valid_ref[...].astype(jnp.float32)
    wide = valid.shape[0]
    pick = ints((rows, wide), 1) == mine * stations + ints((rows, wide), 0) // windows
    own = exact_dot(pick.astype(jnp.float32), valid)
    here = ints(own.shape, 1) == lax.rem(ints(own.shape, 0), windows)
    own = jnp.sum(jnp.where(here, own, 0.0), axis=1, keepdims=True)
    sides = members * SPLIT
    pick = ints((sides, wide), 1) == half * ints((sides, wide), 0) + mine // stations
    held[...] = exact_dot(pick.astype(jnp.float32), valid)
    pick = ints((members, wide), 1) == stations * ints((members, wide), 0) + lax.rem(mine, stations)
    valid_right = exact_dot(pick.astype(jnp.float32), valid)
    owners = owners_ref[...]
    blocks = owners.shape[1]
    owned = (ints((groups, blocks), 0) == owners).astype(jnp.float32)
    earlier = (ints((blocks, blocks), 0) < ints((blocks, blocks), 1)).astype(jnp.float32)
    rank = exact_dot(owned, earlier)
    ontos = []
    for slot in range(CAP):
        chosen = jnp.where(jnp.abs(rank - slot) < 0.5, owned, 0.0)
        onto = jnp.dot(
            chosen.astype(jnp.bfloat16), spread_ref[...], preferred_element_type=jnp.float32
        )
        ontos.append(onto.astype(jnp.bfloat16))

    whole[...] = jnp.zeros_like(whole)
    load.wait()

    @pl.loop(0, SEG // NB)
    def _(step):
        at = pl.ds(pl.multiple_of(step * NB, NB), NB)
        block = raw[:, :, at].reshape(rows * phases, NB)
        upper = block.astype(jnp.bfloat16)
        lower = (block - upper.astype(jnp.float32)).astype(jnp.bfloat16)
        table = waves[at, :]
        total = jnp.dot(upper, table, preferred_element_type=jnp.float32)
        total = total + jnp.dot(upper, rest[at, :], preferred_element_type=jnp.float32)
        total = total + jnp.dot(lower, table, preferred_element_type=jnp.float32)
        whole[...] += total

    whole_re, whole_im = whole[:, :NB], whole[:, NB:]
    gain_re, gain_im = gains[:, :NB], gains[:, NB:]
    join = (ints((rows, rows * phases), 1) // phases == ints((rows, rows * phases), 0)).astype(jnp.float32)
    real = exact_dot(join, whole_re * gain_re - whole_im * gain_im + fix[:, :NB])
    imag = exact_dot(join, whole_re * gain_im + whole_im * gain_re + fix[:, NB:])
    smoothed = exact_dot(real * real + imag * imag, smooth_ref[...])
    whitener = own / jnp.sqrt(smoothed + EPSILON)
    white[:, :, :NB] = (real * whitener).astype(jnp.bfloat16).reshape(stations, windows, NB)
    white[:, :, NB:] = (imag * whitener).astype(jnp.bfloat16).reshape(stations, windows, NB)

    def near(k):
        peer = lax.rem(mine + k, members)
        side_a, side_c = peer // stations, lax.rem(peer, stations)
        copies = []
        for part in range(SPLIT + 1):
            station = side_c if part == SPLIT else part * half + side_a
            into = right.at[mine] if part == SPLIT else left.at[mine, part]
            copies.append(
                pltpu.make_async_remote_copy(
                    src_ref=white.at[station],
                    dst_ref=into,
                    send_sem=near_send.at[k, part],
                    recv_sem=near_recv.at[k, part],
                    device_id={"sta": peer},
                    device_id_type=pl.DeviceIdType.MESH,
                )
            )
        return copies

    pl.semaphore_wait(barrier, members - 1 + groups - 1)
    for k in range(1, members):
        for copy in near(k):
            copy.start()
    for part in range(SPLIT):
        left[mine, part] = white[part * half + mine // stations]
    right[mine] = white[lax.rem(mine, stations)]
    for k in range(1, members):
        for copy in near(k):
            copy.wait()

    @pl.loop(0, members * SPLIT)
    def _(n):
        i, h = n // SPLIT, lax.rem(n, SPLIT)
        ours = left[i, h].astype(jnp.float32)
        theirs = right[...].astype(jnp.float32)
        lr, li = ours[None, :, :NB], ours[None, :, NB:]
        rr, ri = theirs[:, :, :NB], theirs[:, :, NB:]
        rows = pl.ds(pl.multiple_of(n * members, members), members)
        count = jnp.sum(held[pl.ds(n, 1), :] * valid_right, axis=1, keepdims=True)
        scale = 1.0 / (math.sqrt(NB) * jnp.maximum(count, 1.0))
        stack[rows, :NB] = jnp.sum(lr * rr + li * ri, axis=1) * scale
        stack[rows, NB:] = jnp.sum(li * rr - lr * ri, axis=1) * scale

    lead_re, lead_im = lead_ref[0:1], lead_ref[1:2]
    stack_re, stack_im = stack[:, :NB], stack[:, NB:]
    moved_re = (stack_re * lead_re - stack_im * lead_im).astype(jnp.bfloat16)
    moved_im = (stack_re * lead_im + stack_im * lead_re).astype(jnp.bfloat16)
    for slot in range(CAP):
        for part, moved in enumerate((moved_re, moved_im)):
            placed = jnp.dot(ontos[slot], moved, preferred_element_type=jnp.float32)
            for chunk in range(NB // 128):
                row = slot * (2 * NB // 128) + part * (NB // 128) + chunk
                staged[:, row, :] = placed[:, chunk * 128 : (chunk + 1) * 128]
    routed[...] = staged[...].astype(jnp.bfloat16)

    def far(k):
        peer = lax.rem(group + k, groups)
        return pltpu.make_async_remote_copy(
            src_ref=routed.at[peer],
            dst_ref=arrived.at[group],
            send_sem=far_send.at[k],
            recv_sem=far_recv.at[k],
            device_id={"grp": peer},
            device_id_type=pl.DeviceIdType.MESH,
        )

    @pl.loop(1, groups)
    def _(k):
        far(k).start()

    arrived[group] = routed[group]

    @pl.loop(1, groups)
    def _(k):
        far(k).wait()

    out_ref[...] = arrived[...]


def local(seismograms, fir_taps, valid_windows, pair_owners):
    stations, windows, phases, samples = seismograms.shape
    members = lax.axis_size("sta")
    groups = lax.axis_size("grp")
    taps = fir_taps.shape[1]
    rows = stations * windows
    combos = members * SPLIT * members
    raw = seismograms.reshape(rows, phases, samples)
    spare = jnp.zeros((stations, windows, phases, 64 - (taps - 1)), jnp.float32)
    head, tail = seismograms[..., : taps - 1], seismograms[..., SEG:]
    ends = jnp.concatenate([head, spare, tail, spare], axis=-1).reshape(rows * phases, 128)
    phase_taps = jnp.tile(fir_taps, (rows, 1))
    coarse, fine = wave_steps()
    adv, edges = edge_waves(taps)
    lead = np.concatenate(turn([MAXLAG]))
    spread = jnp.asarray(pair_spread(members), jnp.bfloat16)

    vmem = pl.BlockSpec(memory_space=pltpu.VMEM)
    tile = (groups, CAP * 2 * NB // 128, 128)
    arrived, waves = pl.pallas_call(
        functools.partial(combine, members, groups, stations, windows, phases),
        out_shape=(
            jax.ShapeDtypeStruct(tile, jnp.bfloat16),
            jax.ShapeDtypeStruct((SEG, 2 * NB), jnp.bfloat16),
        ),
        in_specs=[pl.BlockSpec(memory_space=pl.ANY)] + [vmem] * 11,
        out_specs=(vmem, vmem),
        scratch_shapes=[
            pltpu.VMEM((rows, phases, samples), jnp.float32),
            pltpu.VMEM((SEG, 2 * NB), jnp.bfloat16),
            pltpu.VMEM((rows * phases, 2 * NB), jnp.float32),
            pltpu.VMEM((stations, windows, 2 * NB), jnp.bfloat16),
            pltpu.VMEM((members, SPLIT, windows, 2 * NB), jnp.bfloat16),
            pltpu.VMEM((members, windows, 2 * NB), jnp.bfloat16),
            pltpu.VMEM((combos, 2 * NB), jnp.float32),
            pltpu.VMEM((members * SPLIT, windows), jnp.float32),
            pltpu.VMEM(tile, jnp.float32),
            pltpu.VMEM(tile, jnp.bfloat16),
            pltpu.VMEM(tile, jnp.bfloat16),
            pltpu.SemaphoreType.DMA,
            pltpu.SemaphoreType.DMA((members, SPLIT + 1)),
            pltpu.SemaphoreType.DMA((members, SPLIT + 1)),
            pltpu.SemaphoreType.DMA((groups,)),
            pltpu.SemaphoreType.DMA((groups,)),
        ],
        compiler_params=pltpu.CompilerParams(collective_id=0, has_side_effects=True),
        name="combine",
    )(
        raw,
        ends,
        phase_taps,
        valid_windows,
        pair_owners.reshape(1, -1),
        coarse,
        fine,
        adv,
        edges,
        smoother(),
        lead,
        spread,
    )
    lagged = lax.dot_general(
        arrived.reshape(groups * CAP, 2 * NB),
        waves[: 2 * MAXLAG + 1],
        (((1,), (1,)), ((), ())),
        preferred_element_type=jnp.float32,
    )
    return lagged.reshape(1, groups, CAP, 1, 2 * MAXLAG + 1)


def solution(mesh):
    in_specs = (P(("grp", "sta"), None, None, None), P(), P("grp", None), P("grp", None, None))
    out_specs = P("grp", None, None, "sta", None)
    return jax.shard_map(local, mesh=mesh, in_specs=in_specs, out_specs=out_specs, check_vma=False)
```

```python
import functools
import math

import jax
import jax.numpy as jnp
import numpy as np
from jax import lax
from jax.experimental import pallas as pl
from jax.experimental.pallas import tpu as pltpu
from jax.sharding import PartitionSpec as P

SEG = 2048
NB = 256
K0 = 16
SMOOTH = 32
MAXLAG = 1000
CAP = 2
SPLIT = 2
STEP = 64

EPSILON = 1e-06
PRECISE = lax.Precision.HIGHEST
FREQS = K0 + np.arange(NB)


def turn(multiples):
    angle = (np.asarray(multiples)[:, None] * FREQS[None, :] % (2 * SEG)) * (math.pi / SEG)
    return np.cos(angle).astype(np.float32), (-np.sin(angle)).astype(np.float32)


def wave_steps():
    coarse = np.concatenate(turn(STEP * np.arange(SEG // STEP)), axis=1)
    fine = np.concatenate(turn(np.arange(STEP)), axis=1)
    return coarse, fine


def smoother():
    near = np.abs(np.arange(NB)[:, None] - np.arange(NB)[None, :]) <= SMOOTH
    return near.astype(np.float32) / (2 * SMOOTH + 1)


def edge_waves(taps):
    adv = np.concatenate(turn(-np.arange(taps)), axis=1)
    sign = np.where(FREQS % 2 == 0, 1.0, -1.0).astype(np.float32)
    edges = np.zeros((128, 2 * NB), np.float32)
    for j in range(1, taps):
        edges[128 - j] = -adv[j]
        edges[64 - j] = adv[j] * np.concatenate([sign, sign])
    return adv, edges


def pair_spread(members):
    rows_of, cols_of = np.triu_indices(members)
    pair_i = np.repeat(rows_of, SPLIT)
    pair_j = np.repeat(cols_of, SPLIT)
    pair_h = np.tile(np.arange(SPLIT), rows_of.shape[0])
    combo_of = (pair_i * SPLIT + pair_h) * members + pair_j
    spread = np.zeros((combo_of.size, members * SPLIT * members), np.float32)
    spread[np.arange(combo_of.size), combo_of] = 1.0
    return spread


def ints(shape, axis):
    return lax.broadcasted_iota(jnp.int32, shape, axis)


def exact_dot(a, b):
    return jnp.dot(a, b, precision=PRECISE, preferred_element_type=jnp.float32)


def exact_dot_t(a, b):
    return lax.dot_general(
        a, b, (((1,), (1,)), ((), ())), precision=PRECISE, preferred_element_type=jnp.float32
    )


def combine(members, groups, stations, windows, phases, *refs):
    (raw_hbm, taps_ref, valid_ref, owners_ref) = refs[:4]
    (coarse_ref, fine_ref, adv_ref, edge_ref, smooth_ref, lead_ref, spread_ref) = refs[4:11]
    out_ref = refs[11]
    (raw, waves, rest, whole, white, left, right, stack, held, staged, routed, arrived) = refs[12:24]
    raw_sem, near_send, near_recv, far_send, far_recv = refs[24:]
    mine = lax.axis_index("sta")
    group = lax.axis_index("grp")
    half = stations // SPLIT
    rows = stations * windows

    load = pltpu.make_async_copy(raw_hbm, raw, raw_sem)
    load.start()
    barrier = pltpu.get_barrier_semaphore()

    @pl.loop(1, groups, unroll=7)
    def _(k):
        pl.semaphore_signal(
            barrier,
            inc=1,
            device_id={"grp": lax.rem(group + k, groups)},
            device_id_type=pl.DeviceIdType.MESH,
        )

    @pl.loop(1, members)
    def _(k):
        pl.semaphore_signal(
            barrier,
            inc=1,
            device_id={"sta": lax.rem(mine + k, members)},
            device_id_type=pl.DeviceIdType.MESH,
        )

    @pl.loop(0, SEG // STEP)
    def _(step):
        at = pl.ds(pl.multiple_of(step * STEP, STEP), STEP)
        cr, ci = coarse_ref[pl.ds(step, 1), :NB], coarse_ref[pl.ds(step, 1), NB:]
        fr, fi = fine_ref[:, :NB], fine_ref[:, NB:]
        for part, wave in enumerate((cr * fr - ci * fi, cr * fi + ci * fr)):
            upper = wave.astype(jnp.bfloat16)
            waves[at, part * NB : (part + 1) * NB] = upper
            lower = (wave - upper.astype(jnp.float32)).astype(jnp.bfloat16)
            rest[at, part * NB : (part + 1) * NB] = lower

    pick = ints((rows * phases, phases), 1) == lax.rem(ints((rows * phases, phases), 0), phases)
    phase_taps = exact_dot(pick.astype(jnp.float32), taps_ref[...])
    taps = phase_taps.shape[1]
    gains = exact_dot(phase_taps, adv_ref[...])
    valid = valid_ref[...].astype(jnp.float32)
    wide = valid.shape[1]
    pick = ints((rows, wide), 1) == mine * stations + ints((rows, wide), 0) // windows
    own = exact_dot_t(pick.astype(jnp.float32), valid)
    here = ints(own.shape, 1) == lax.rem(ints(own.shape, 0), windows)
    own = jnp.sum(jnp.where(here, own, 0.0), axis=1, keepdims=True)
    sides = members * SPLIT
    pick = ints((sides, wide), 1) == half * ints((sides, wide), 0) + mine // stations
    held[...] = exact_dot_t(pick.astype(jnp.float32), valid)
    pick = ints((members, wide), 1) == stations * ints((members, wide), 0) + lax.rem(mine, stations)
    valid_right = exact_dot_t(pick.astype(jnp.float32), valid)
    owners = owners_ref[...]
    blocks = owners.shape[1]
    owned = (ints((groups, blocks), 0) == owners).astype(jnp.float32)
    earlier = (ints((blocks, blocks), 0) < ints((blocks, blocks), 1)).astype(jnp.float32)
    rank = exact_dot(owned, earlier)
    ontos = []
    for slot in range(CAP):
        chosen = jnp.where(jnp.abs(rank - slot) < 0.5, owned, 0.0)
        onto = jnp.dot(
            chosen.astype(jnp.bfloat16), spread_ref[...], preferred_element_type=jnp.float32
        )
        ontos.append(onto.astype(jnp.bfloat16))

    load.wait()
    lanes = ints((rows * phases, 128), 1)
    head = raw[:, :, :128].reshape(rows * phases, 128)
    tail = raw[:, :, SEG + taps - 1 - 128 :].reshape(rows * phases, 128)
    tail = pltpu.roll(jnp.where(lanes > 128 - taps, tail, 0.0), 64 + taps - 1, 1)
    ends = jnp.where(lanes < taps - 1, head, tail)
    past = ends * phase_taps[:, 0:1]
    for q in range(1, taps):
        past = past + pltpu.roll(ends, 128 - q, 1) * phase_taps[:, q : q + 1]
    fix = exact_dot(past, edge_ref[...])
    whole[...] = jnp.zeros_like(whole)

    @pl.loop(0, SEG // NB)
    def _(step):
        at = pl.ds(pl.multiple_of(step * NB, NB), NB)
        block = raw[:, :, at].reshape(rows * phases, NB)
        upper = block.astype(jnp.bfloat16)
        lower = (block - upper.astype(jnp.float32)).astype(jnp.bfloat16)
        table = waves[at, :]
        total = jnp.dot(upper, table, preferred_element_type=jnp.float32)
        total = total + jnp.dot(upper, rest[at, :], preferred_element_type=jnp.float32)
        total = total + jnp.dot(lower, table, preferred_element_type=jnp.float32)
        whole[...] += total

    whole_re, whole_im = whole[:, :NB], whole[:, NB:]
    gain_re, gain_im = gains[:, :NB], gains[:, NB:]
    join = (ints((rows, rows * phases), 1) // phases == ints((rows, rows * phases), 0)).astype(jnp.float32)
    real = exact_dot(join, whole_re * gain_re - whole_im * gain_im + fix[:, :NB])
    imag = exact_dot(join, whole_re * gain_im + whole_im * gain_re + fix[:, NB:])
    smoothed = exact_dot(real * real + imag * imag, smooth_ref[...])
    whitener = own / jnp.sqrt(smoothed + EPSILON)
    white[:, :, :NB] = (real * whitener).astype(jnp.bfloat16).reshape(stations, windows, NB)
    white[:, :, NB:] = (imag * whitener).astype(jnp.bfloat16).reshape(stations, windows, NB)

    def near(k):
        peer = lax.rem(mine + k, members)
        side_a, side_c = peer // stations, lax.rem(peer, stations)
        copies = []
        for part in range(SPLIT + 1):
            station = side_c if part == SPLIT else part * half + side_a
            into = right.at[mine] if part == SPLIT else left.at[mine, part]
            copies.append(
                pltpu.make_async_remote_copy(
                    src_ref=white.at[station],
                    dst_ref=into,
                    send_sem=near_send.at[k, part],
                    recv_sem=near_recv.at[k, part],
                    device_id={"sta": peer},
                    device_id_type=pl.DeviceIdType.MESH,
                )
            )
        return copies

    pl.semaphore_wait(barrier, members - 1 + groups - 1)
    for k in range(1, members):
        for copy in near(k):
            copy.start()
    for part in range(SPLIT):
        left[mine, part] = white[part * half + mine // stations]
    right[mine] = white[lax.rem(mine, stations)]
    for k in range(1, members):
        for copy in near(k):
            copy.wait()

    @pl.loop(0, members * SPLIT, unroll=4)
    def _(n):
        i, h = n // SPLIT, lax.rem(n, SPLIT)
        ours = left[i, h].astype(jnp.float32)
        theirs = right[...].astype(jnp.float32)
        lr, li = ours[None, :, :NB], ours[None, :, NB:]
        rr, ri = theirs[:, :, :NB], theirs[:, :, NB:]
        rows = pl.ds(pl.multiple_of(n * members, members), members)
        count = jnp.sum(held[pl.ds(n, 1), :] * valid_right, axis=1, keepdims=True)
        scale = 1.0 / (math.sqrt(NB) * jnp.maximum(count, 1.0))
        stack[rows, :NB] = jnp.sum(lr * rr + li * ri, axis=1) * scale
        stack[rows, NB:] = jnp.sum(li * rr - lr * ri, axis=1) * scale

    lead_re, lead_im = lead_ref[0:1], lead_ref[1:2]
    stack_re, stack_im = stack[:, :NB], stack[:, NB:]
    moved_re = (stack_re * lead_re - stack_im * lead_im).astype(jnp.bfloat16)
    moved_im = (stack_re * lead_im + stack_im * lead_re).astype(jnp.bfloat16)
    for slot in range(CAP):
        for part, moved in enumerate((moved_re, moved_im)):
            placed = jnp.dot(ontos[slot], moved, preferred_element_type=jnp.float32)
            for chunk in range(NB // 128):
                row = slot * (2 * NB // 128) + part * (NB // 128) + chunk
                staged[:, row, :] = placed[:, chunk * 128 : (chunk + 1) * 128]
    routed[...] = staged[...].astype(jnp.bfloat16)

    def far(k):
        peer = lax.rem(group + k, groups)
        return pltpu.make_async_remote_copy(
            src_ref=routed.at[peer],
            dst_ref=arrived.at[group],
            send_sem=far_send.at[k],
            recv_sem=far_recv.at[k],
            device_id={"grp": peer},
            device_id_type=pl.DeviceIdType.MESH,
        )

    @pl.loop(1, groups, unroll=7)
    def _(k):
        far(k).start()

    arrived[group] = routed[group]

    @pl.loop(1, groups, unroll=7)
    def _(k):
        far(k).wait()

    out_ref[...] = arrived[...]


def to_lags(arrived_ref, coarse_ref, fine_ref, out_ref, staged):
    staged[...] = arrived_ref[...].astype(jnp.float32)
    chunks = 2 * NB // 128
    sides = []
    for slot in range(CAP):
        parts = [staged[:, slot * chunks + c, :] for c in range(chunks)]
        sides.append(jnp.concatenate(parts, axis=1))
    stacks = jnp.concatenate(sides, axis=0).astype(jnp.bfloat16)
    groups = arrived_ref.shape[0]
    fr, fi = fine_ref[:, :NB], fine_ref[:, NB:]
    lags = out_ref.shape[-1]
    wide = 2 * STEP
    for first in range(0, lags, wide):
        real, imag = [], []
        for step in range(first // STEP, (first + wide) // STEP):
            cr, ci = coarse_ref[step : step + 1, :NB], coarse_ref[step : step + 1, NB:]
            real.append((cr * fr - ci * fi).astype(jnp.bfloat16))
            imag.append((cr * fi + ci * fr).astype(jnp.bfloat16))
        table = jnp.concatenate(
            [jnp.concatenate(real, axis=0), jnp.concatenate(imag, axis=0)], axis=1
        )
        block = lax.dot_general(
            stacks, table, (((1,), (1,)), ((), ())), preferred_element_type=jnp.float32
        )
        width = min(wide, lags - first)
        for slot in range(CAP):
            out_ref[:, slot, 0, first : first + width] = block[
                slot * groups : (slot + 1) * groups, :width
            ]


def local(seismograms, fir_taps, valid_windows, pair_owners):
    stations, windows, phases, samples = seismograms.shape
    members = lax.axis_size("sta")
    groups = lax.axis_size("grp")
    taps = fir_taps.shape[1]
    rows = stations * windows
    combos = members * SPLIT * members
    raw = seismograms.reshape(rows, phases, samples)
    coarse, fine = wave_steps()
    adv, edges = edge_waves(taps)
    lead = np.concatenate(turn([MAXLAG]))
    spread = jnp.asarray(pair_spread(members), jnp.bfloat16)

    vmem = pl.BlockSpec(memory_space=pltpu.VMEM)
    tile = (groups, CAP * 2 * NB // 128, 128)
    arrived = pl.pallas_call(
        functools.partial(combine, members, groups, stations, windows, phases),
        out_shape=jax.ShapeDtypeStruct(tile, jnp.bfloat16),
        in_specs=[pl.BlockSpec(memory_space=pl.ANY)] + [vmem] * 10,
        out_specs=vmem,
        scratch_shapes=[
            pltpu.VMEM((rows, phases, samples), jnp.float32),
            pltpu.VMEM((SEG, 2 * NB), jnp.bfloat16),
            pltpu.VMEM((SEG, 2 * NB), jnp.bfloat16),
            pltpu.VMEM((rows * phases, 2 * NB), jnp.float32),
            pltpu.VMEM((stations, windows, 2 * NB), jnp.bfloat16),
            pltpu.VMEM((members, SPLIT, windows, 2 * NB), jnp.bfloat16),
            pltpu.VMEM((members, windows, 2 * NB), jnp.bfloat16),
            pltpu.VMEM((combos, 2 * NB), jnp.float32),
            pltpu.VMEM((members * SPLIT, windows), jnp.float32),
            pltpu.VMEM(tile, jnp.float32),
            pltpu.VMEM(tile, jnp.bfloat16),
            pltpu.VMEM(tile, jnp.bfloat16),
            pltpu.SemaphoreType.DMA,
            pltpu.SemaphoreType.DMA((members, SPLIT + 1)),
            pltpu.SemaphoreType.DMA((members, SPLIT + 1)),
            pltpu.SemaphoreType.DMA((groups,)),
            pltpu.SemaphoreType.DMA((groups,)),
        ],
        compiler_params=pltpu.CompilerParams(collective_id=0, has_side_effects=True),
        name="combine",
    )(
        raw,
        fir_taps,
        valid_windows.T,
        pair_owners.reshape(1, -1),
        coarse,
        fine,
        adv,
        edges,
        smoother(),
        lead,
        spread,
    )
    lagged = pl.pallas_call(
        to_lags,
        out_shape=jax.ShapeDtypeStruct((groups, CAP, 1, 2 * MAXLAG + 1), jnp.float32),
        in_specs=[vmem] * 3,
        out_specs=vmem,
        scratch_shapes=[pltpu.VMEM(tile, jnp.float32)],
        name="to_lags",
    )(arrived, coarse, fine)
    return lagged[None, :, :, :, :]


def solution(mesh):
    in_specs = (P(("grp", "sta"), None, None, None), P(), P("grp", None), P("grp", None, None))
    out_specs = P("grp", None, None, "sta", None)
    return jax.shard_map(local, mesh=mesh, in_specs=in_specs, out_specs=out_specs, check_vma=False)
```

```python
import functools
import math

import jax
import jax.numpy as jnp
import numpy as np
from jax import lax
from jax.experimental import pallas as pl
from jax.experimental.pallas import tpu as pltpu
from jax.sharding import PartitionSpec as P

SEG = 2048
NB = 256
K0 = 16
SMOOTH = 32
MAXLAG = 1000
CAP = 2
SPLIT = 2
STEP = 64
INNER = 8

EPSILON = 1e-06
PRECISE = lax.Precision.HIGHEST
FREQS = K0 + np.arange(NB)


def turn(multiples):
    angle = (np.asarray(multiples)[:, None] * FREQS[None, :] % (2 * SEG)) * (math.pi / SEG)
    return np.cos(angle).astype(np.float32), (-np.sin(angle)).astype(np.float32)


def wave_steps():
    coarse = np.concatenate(turn(STEP * np.arange(SEG // STEP)), axis=1)
    fine = np.concatenate(turn(np.arange(STEP)), axis=1)
    return coarse, fine


def smoother():
    near = np.abs(np.arange(NB)[:, None] - np.arange(NB)[None, :]) <= SMOOTH
    return near.astype(np.float32) / (2 * SMOOTH + 1)


def edge_waves(taps):
    adv = np.concatenate(turn(-np.arange(taps)), axis=1)
    sign = np.where(FREQS % 2 == 0, 1.0, -1.0).astype(np.float32)
    edges = np.zeros((128, 2 * NB), np.float32)
    for j in range(1, taps):
        edges[128 - j] = -adv[j]
        edges[64 - j] = adv[j] * np.concatenate([sign, sign])
    return adv, edges


def pair_spread(members):
    rows_of, cols_of = np.triu_indices(members)
    pair_i = np.repeat(rows_of, SPLIT)
    pair_j = np.repeat(cols_of, SPLIT)
    pair_h = np.tile(np.arange(SPLIT), rows_of.shape[0])
    combo_of = (pair_i * SPLIT + pair_h) * members + pair_j
    spread = np.zeros((combo_of.size, members * SPLIT * members), np.float32)
    spread[np.arange(combo_of.size), combo_of] = 1.0
    return spread


def ints(shape, axis):
    return lax.broadcasted_iota(jnp.int32, shape, axis)


def exact_dot(a, b):
    return jnp.dot(a, b, precision=PRECISE, preferred_element_type=jnp.float32)


def exact_dot_t(a, b):
    return lax.dot_general(
        a, b, (((1,), (1,)), ((), ())), precision=PRECISE, preferred_element_type=jnp.float32
    )


def combine(members, groups, stations, windows, phases, *refs):
    (raw_hbm, taps_ref, valid_ref, owners_ref) = refs[:4]
    (coarse_ref, fine_ref, adv_ref, edge_ref, smooth_ref, lead_ref, spread_ref) = refs[4:11]
    out_ref = refs[11]
    (raw, waves, rest, whole, white, left, right, stack, held, staged, routed) = refs[12:23]
    passing, arrived, raw_sem, near_send, near_recv, far_send, far_recv = refs[23:]
    mine = lax.axis_index("sta")
    group = lax.axis_index("grp")
    half = stations // SPLIT
    rows = stations * windows

    load = pltpu.make_async_copy(raw_hbm, raw, raw_sem)
    load.start()
    barrier = pltpu.get_barrier_semaphore()

    inner = min(INNER, groups)
    outer = groups // inner
    line, place = group // inner, lax.rem(group, inner)

    def greet(peer):
        pl.semaphore_signal(barrier, inc=1, device_id=peer, device_id_type=pl.DeviceIdType.MESH)

    for k in range(1, outer):
        greet({"grp": lax.rem(line + k, outer) * inner + place})
    for k in range(1, inner):
        greet({"grp": line * inner + lax.rem(place + k, inner)})
    for k in range(1, members):
        greet({"sta": lax.rem(mine + k, members)})

    @pl.loop(0, SEG // STEP)
    def _(step):
        at = pl.ds(pl.multiple_of(step * STEP, STEP), STEP)
        cr, ci = coarse_ref[pl.ds(step, 1), :NB], coarse_ref[pl.ds(step, 1), NB:]
        fr, fi = fine_ref[:, :NB], fine_ref[:, NB:]
        for part, wave in enumerate((cr * fr - ci * fi, cr * fi + ci * fr)):
            upper = wave.astype(jnp.bfloat16)
            waves[at, part * NB : (part + 1) * NB] = upper
            lower = (wave - upper.astype(jnp.float32)).astype(jnp.bfloat16)
            rest[at, part * NB : (part + 1) * NB] = lower

    pick = ints((rows * phases, phases), 1) == lax.rem(ints((rows * phases, phases), 0), phases)
    phase_taps = exact_dot(pick.astype(jnp.float32), taps_ref[...])
    taps = phase_taps.shape[1]
    gains = exact_dot(phase_taps, adv_ref[...])
    valid = valid_ref[...].astype(jnp.float32)
    wide = valid.shape[1]
    pick = ints((rows, wide), 1) == mine * stations + ints((rows, wide), 0) // windows
    own = exact_dot_t(pick.astype(jnp.float32), valid)
    here = ints(own.shape, 1) == lax.rem(ints(own.shape, 0), windows)
    own = jnp.sum(jnp.where(here, own, 0.0), axis=1, keepdims=True)
    sides = members * SPLIT
    pick = ints((sides, wide), 1) == half * ints((sides, wide), 0) + mine // stations
    held[...] = exact_dot_t(pick.astype(jnp.float32), valid)
    pick = ints((members, wide), 1) == stations * ints((members, wide), 0) + lax.rem(mine, stations)
    valid_right = exact_dot_t(pick.astype(jnp.float32), valid)
    owners = owners_ref[...]
    blocks = owners.shape[1]
    named = ints((groups, blocks), 0)
    named = lax.rem(named, outer) * inner + named // outer
    owned = (named == owners).astype(jnp.float32)
    earlier = (ints((blocks, blocks), 0) < ints((blocks, blocks), 1)).astype(jnp.float32)
    rank = exact_dot(owned, earlier)
    ontos = []
    for slot in range(CAP):
        chosen = jnp.where(jnp.abs(rank - slot) < 0.5, owned, 0.0)
        onto = jnp.dot(
            chosen.astype(jnp.bfloat16), spread_ref[...], preferred_element_type=jnp.float32
        )
        ontos.append(onto.astype(jnp.bfloat16))

    load.wait()
    lanes = ints((rows * phases, 128), 1)
    head = raw[:, :, :128].reshape(rows * phases, 128)
    tail = raw[:, :, SEG + taps - 1 - 128 :].reshape(rows * phases, 128)
    tail = pltpu.roll(jnp.where(lanes > 128 - taps, tail, 0.0), 64 + taps - 1, 1)
    ends = jnp.where(lanes < taps - 1, head, tail)
    past = ends * phase_taps[:, 0:1]
    for q in range(1, taps):
        past = past + pltpu.roll(ends, 128 - q, 1) * phase_taps[:, q : q + 1]
    fix = exact_dot(past, edge_ref[...])
    whole[...] = jnp.zeros_like(whole)

    @pl.loop(0, SEG // NB)
    def _(step):
        at = pl.ds(pl.multiple_of(step * NB, NB), NB)
        block = raw[:, :, at].reshape(rows * phases, NB)
        upper = block.astype(jnp.bfloat16)
        lower = (block - upper.astype(jnp.float32)).astype(jnp.bfloat16)
        table = waves[at, :]
        total = jnp.dot(upper, table, preferred_element_type=jnp.float32)
        total = total + jnp.dot(upper, rest[at, :], preferred_element_type=jnp.float32)
        total = total + jnp.dot(lower, table, preferred_element_type=jnp.float32)
        whole[...] += total

    whole_re, whole_im = whole[:, :NB], whole[:, NB:]
    gain_re, gain_im = gains[:, :NB], gains[:, NB:]
    join = (ints((rows, rows * phases), 1) // phases == ints((rows, rows * phases), 0)).astype(jnp.float32)
    real = exact_dot(join, whole_re * gain_re - whole_im * gain_im + fix[:, :NB])
    imag = exact_dot(join, whole_re * gain_im + whole_im * gain_re + fix[:, NB:])
    smoothed = exact_dot(real * real + imag * imag, smooth_ref[...])
    whitener = own / jnp.sqrt(smoothed + EPSILON)
    white[:, :, :NB] = (real * whitener).astype(jnp.bfloat16).reshape(stations, windows, NB)
    white[:, :, NB:] = (imag * whitener).astype(jnp.bfloat16).reshape(stations, windows, NB)

    def near(k):
        peer = lax.rem(mine + k, members)
        side_a, side_c = peer // stations, lax.rem(peer, stations)
        copies = []
        for part in range(SPLIT + 1):
            station = side_c if part == SPLIT else part * half + side_a
            into = right.at[mine] if part == SPLIT else left.at[mine, part]
            copies.append(
                pltpu.make_async_remote_copy(
                    src_ref=white.at[station],
                    dst_ref=into,
                    send_sem=near_send.at[k, part],
                    recv_sem=near_recv.at[k, part],
                    device_id={"sta": peer},
                    device_id_type=pl.DeviceIdType.MESH,
                )
            )
        return copies

    pl.semaphore_wait(barrier, members - 1 + inner - 1 + outer - 1)
    for k in range(1, members):
        for copy in near(k):
            copy.start()
    for part in range(SPLIT):
        left[mine, part] = white[part * half + mine // stations]
    right[mine] = white[lax.rem(mine, stations)]
    for k in range(1, members):
        for copy in near(k):
            copy.wait()

    @pl.loop(0, members * SPLIT, unroll=4)
    def _(n):
        i, h = n // SPLIT, lax.rem(n, SPLIT)
        ours = left[i, h].astype(jnp.float32)
        theirs = right[...].astype(jnp.float32)
        lr, li = ours[None, :, :NB], ours[None, :, NB:]
        rr, ri = theirs[:, :, :NB], theirs[:, :, NB:]
        rows = pl.ds(pl.multiple_of(n * members, members), members)
        count = jnp.sum(held[pl.ds(n, 1), :] * valid_right, axis=1, keepdims=True)
        scale = 1.0 / (math.sqrt(NB) * jnp.maximum(count, 1.0))
        stack[rows, :NB] = jnp.sum(lr * rr + li * ri, axis=1) * scale
        stack[rows, NB:] = jnp.sum(li * rr - lr * ri, axis=1) * scale

    lead_re, lead_im = lead_ref[0:1], lead_ref[1:2]
    stack_re, stack_im = stack[:, :NB], stack[:, NB:]
    moved_re = (stack_re * lead_re - stack_im * lead_im).astype(jnp.bfloat16)
    moved_im = (stack_re * lead_im + stack_im * lead_re).astype(jnp.bfloat16)
    for slot in range(CAP):
        for part, moved in enumerate((moved_re, moved_im)):
            placed = jnp.dot(ontos[slot], moved, preferred_element_type=jnp.float32)
            for chunk in range(NB // 128):
                row = slot * (2 * NB // 128) + part * (NB // 128) + chunk
                staged[:, row, :] = placed[:, chunk * 128 : (chunk + 1) * 128]
    routed[...] = staged[...].astype(jnp.bfloat16).reshape(routed.shape)

    def along(k):
        peer = lax.rem(place + k, inner)
        return pltpu.make_async_remote_copy(
            src_ref=routed.at[peer],
            dst_ref=passing.at[place],
            send_sem=far_send.at[k],
            recv_sem=far_recv.at[k],
            device_id={"grp": line * inner + peer},
            device_id_type=pl.DeviceIdType.MESH,
        )

    def across(k):
        peer = lax.rem(line + k, outer)
        return pltpu.make_async_remote_copy(
            src_ref=passing.at[:, peer],
            dst_ref=arrived.at[line],
            send_sem=far_send.at[inner + k],
            recv_sem=far_recv.at[inner + k],
            device_id={"grp": peer * inner + place},
            device_id_type=pl.DeviceIdType.MESH,
        )

    order = sorted(range(1, inner), key=lambda k: -min(k, inner - k))
    for k in order:
        along(k).start()
    passing[place] = routed[place]
    for k in order:
        along(k).wait()
    order = sorted(range(1, outer), key=lambda k: -min(k, outer - k))
    for k in order:
        across(k).start()
    arrived[line] = passing[:, line]
    for k in order:
        across(k).wait()

    out_ref[...] = arrived[...].reshape(out_ref.shape)


def to_lags(arrived_ref, coarse_ref, fine_ref, out_ref, staged):
    staged[...] = arrived_ref[...].astype(jnp.float32)
    chunks = 2 * NB // 128
    sides = []
    for slot in range(CAP):
        parts = [staged[:, slot * chunks + c, :] for c in range(chunks)]
        sides.append(jnp.concatenate(parts, axis=1))
    stacks = jnp.concatenate(sides, axis=0).astype(jnp.bfloat16)
    groups = arrived_ref.shape[0]
    fr, fi = fine_ref[:, :NB], fine_ref[:, NB:]
    lags = out_ref.shape[-1]
    wide = 2 * STEP
    for first in range(0, lags, wide):
        real, imag = [], []
        for step in range(first // STEP, (first + wide) // STEP):
            cr, ci = coarse_ref[step : step + 1, :NB], coarse_ref[step : step + 1, NB:]
            real.append((cr * fr - ci * fi).astype(jnp.bfloat16))
            imag.append((cr * fi + ci * fr).astype(jnp.bfloat16))
        table = jnp.concatenate(
            [jnp.concatenate(real, axis=0), jnp.concatenate(imag, axis=0)], axis=1
        )
        block = lax.dot_general(
            stacks, table, (((1,), (1,)), ((), ())), preferred_element_type=jnp.float32
        )
        width = min(wide, lags - first)
        for slot in range(CAP):
            out_ref[:, slot, 0, first : first + width] = block[
                slot * groups : (slot + 1) * groups, :width
            ]


def local(seismograms, fir_taps, valid_windows, pair_owners):
    stations, windows, phases, samples = seismograms.shape
    members = lax.axis_size("sta")
    groups = lax.axis_size("grp")
    taps = fir_taps.shape[1]
    rows = stations * windows
    combos = members * SPLIT * members
    raw = seismograms.reshape(rows, phases, samples)
    coarse, fine = wave_steps()
    adv, edges = edge_waves(taps)
    lead = np.concatenate(turn([MAXLAG]))
    spread = jnp.asarray(pair_spread(members), jnp.bfloat16)

    vmem = pl.BlockSpec(memory_space=pltpu.VMEM)
    tile = (groups, CAP * 2 * NB // 128, 128)
    inner = min(INNER, groups)
    outer = groups // inner
    arrived = pl.pallas_call(
        functools.partial(combine, members, groups, stations, windows, phases),
        out_shape=jax.ShapeDtypeStruct(tile, jnp.bfloat16),
        in_specs=[pl.BlockSpec(memory_space=pl.ANY)] + [vmem] * 10,
        out_specs=vmem,
        scratch_shapes=[
            pltpu.VMEM((rows, phases, samples), jnp.float32),
            pltpu.VMEM((SEG, 2 * NB), jnp.bfloat16),
            pltpu.VMEM((SEG, 2 * NB), jnp.bfloat16),
            pltpu.VMEM((rows * phases, 2 * NB), jnp.float32),
            pltpu.VMEM((stations, windows, 2 * NB), jnp.bfloat16),
            pltpu.VMEM((members, SPLIT, windows, 2 * NB), jnp.bfloat16),
            pltpu.VMEM((members, windows, 2 * NB), jnp.bfloat16),
            pltpu.VMEM((combos, 2 * NB), jnp.float32),
            pltpu.VMEM((members * SPLIT, windows), jnp.float32),
            pltpu.VMEM(tile, jnp.float32),
            pltpu.VMEM((inner, outer) + tile[1:], jnp.bfloat16),
            pltpu.VMEM((inner, outer) + tile[1:], jnp.bfloat16),
            pltpu.VMEM((outer, inner) + tile[1:], jnp.bfloat16),
            pltpu.SemaphoreType.DMA,
            pltpu.SemaphoreType.DMA((members, SPLIT + 1)),
            pltpu.SemaphoreType.DMA((members, SPLIT + 1)),
            pltpu.SemaphoreType.DMA((inner + outer,)),
            pltpu.SemaphoreType.DMA((inner + outer,)),
        ],
        compiler_params=pltpu.CompilerParams(collective_id=0, has_side_effects=True),
        name="combine",
    )(
        raw,
        fir_taps,
        valid_windows.T,
        pair_owners.reshape(1, -1),
        coarse,
        fine,
        adv,
        edges,
        smoother(),
        lead,
        spread,
    )
    lagged = pl.pallas_call(
        to_lags,
        out_shape=jax.ShapeDtypeStruct((groups, CAP, 1, 2 * MAXLAG + 1), jnp.float32),
        in_specs=[vmem] * 3,
        out_specs=vmem,
        scratch_shapes=[pltpu.VMEM(tile, jnp.float32)],
        name="to_lags",
    )(arrived, coarse, fine)
    return lagged[None, :, :, :, :]


def solution(mesh):
    in_specs = (P(("grp", "sta"), None, None, None), P(), P("grp", None), P("grp", None, None))
    out_specs = P("grp", None, None, "sta", None)
    return jax.shard_map(local, mesh=mesh, in_specs=in_specs, out_specs=out_specs, check_vma=False)
```

```python
import functools
import math

import jax
import jax.numpy as jnp
import numpy as np
from jax import lax
from jax.experimental import pallas as pl
from jax.experimental.pallas import tpu as pltpu
from jax.sharding import PartitionSpec as P

SEG = 2048
NB = 256
K0 = 16
SMOOTH = 32
MAXLAG = 1000
CAP = 2
SPLIT = 2
STEP = 64
INNER = 8

EPSILON = 1e-06
PRECISE = lax.Precision.HIGHEST
FREQS = K0 + np.arange(NB)


def turn(multiples):
    angle = (np.asarray(multiples)[:, None] * FREQS[None, :] % (2 * SEG)) * (math.pi / SEG)
    return np.cos(angle).astype(np.float32), (-np.sin(angle)).astype(np.float32)


def wave_steps():
    coarse = np.concatenate(turn(STEP * np.arange(SEG // STEP)), axis=1)
    fine = np.concatenate(turn(np.arange(STEP)), axis=1)
    return coarse, fine


def smoother():
    near = np.abs(np.arange(NB)[:, None] - np.arange(NB)[None, :]) <= SMOOTH
    return near.astype(np.float32) / (2 * SMOOTH + 1)


def edge_waves(taps):
    adv = np.concatenate(turn(-np.arange(taps)), axis=1)
    sign = np.where(FREQS % 2 == 0, 1.0, -1.0).astype(np.float32)
    edges = np.zeros((128, 2 * NB), np.float32)
    for j in range(1, taps):
        edges[128 - j] = -adv[j]
        edges[64 - j] = adv[j] * np.concatenate([sign, sign])
    return adv, edges


def pair_spread(members):
    rows_of, cols_of = np.triu_indices(members)
    pair_i = np.repeat(rows_of, SPLIT)
    pair_j = np.repeat(cols_of, SPLIT)
    pair_h = np.tile(np.arange(SPLIT), rows_of.shape[0])
    combo_of = (pair_i * SPLIT + pair_h) * members + pair_j
    spread = np.zeros((combo_of.size, members * SPLIT * members), np.float32)
    spread[np.arange(combo_of.size), combo_of] = 1.0
    return spread


def ints(shape, axis):
    return lax.broadcasted_iota(jnp.int32, shape, axis)


def exact_dot(a, b):
    return jnp.dot(a, b, precision=PRECISE, preferred_element_type=jnp.float32)


def exact_dot_t(a, b):
    return lax.dot_general(
        a, b, (((1,), (1,)), ((), ())), precision=PRECISE, preferred_element_type=jnp.float32
    )


def combine(members, groups, stations, windows, phases, *refs):
    (raw_hbm, taps_ref, valid_ref, owners_ref) = refs[:4]
    (coarse_ref, fine_ref, adv_ref, edge_ref, smooth_ref, lead_ref, spread_ref) = refs[4:11]
    out_ref = refs[11]
    (raw, waves, rest, whole, white, left, right, stack, held, staged) = refs[12:22]
    (routed_z, passing_z, arrived_y, routed_y, passing_y, arrived_z) = refs[22:28]
    raw_sem, near_send, near_recv, far_send, far_recv = refs[28:]
    mine = lax.axis_index("sta")
    group = lax.axis_index("grp")
    half = stations // SPLIT
    rows = stations * windows

    load = pltpu.make_async_copy(raw_hbm, raw, raw_sem)
    load.start()
    barrier = pltpu.get_barrier_semaphore()

    inner = min(INNER, groups)
    outer = groups // inner
    line, place = group // inner, lax.rem(group, inner)

    def greet(peer):
        pl.semaphore_signal(barrier, inc=1, device_id=peer, device_id_type=pl.DeviceIdType.MESH)

    for k in range(1, outer):
        greet({"grp": lax.rem(line + k, outer) * inner + place})
    for k in range(1, inner):
        greet({"grp": line * inner + lax.rem(place + k, inner)})
    for k in range(1, members):
        greet({"sta": lax.rem(mine + k, members)})

    @pl.loop(0, SEG // STEP)
    def _(step):
        at = pl.ds(pl.multiple_of(step * STEP, STEP), STEP)
        cr, ci = coarse_ref[pl.ds(step, 1), :NB], coarse_ref[pl.ds(step, 1), NB:]
        fr, fi = fine_ref[:, :NB], fine_ref[:, NB:]
        for part, wave in enumerate((cr * fr - ci * fi, cr * fi + ci * fr)):
            upper = wave.astype(jnp.bfloat16)
            waves[at, part * NB : (part + 1) * NB] = upper
            lower = (wave - upper.astype(jnp.float32)).astype(jnp.bfloat16)
            rest[at, part * NB : (part + 1) * NB] = lower

    pick = ints((rows * phases, phases), 1) == lax.rem(ints((rows * phases, phases), 0), phases)
    phase_taps = exact_dot(pick.astype(jnp.float32), taps_ref[...])
    taps = phase_taps.shape[1]
    gains = exact_dot(phase_taps, adv_ref[...])
    valid = valid_ref[...].astype(jnp.float32)
    wide = valid.shape[1]
    pick = ints((rows, wide), 1) == mine * stations + ints((rows, wide), 0) // windows
    own = exact_dot_t(pick.astype(jnp.float32), valid)
    here = ints(own.shape, 1) == lax.rem(ints(own.shape, 0), windows)
    own = jnp.sum(jnp.where(here, own, 0.0), axis=1, keepdims=True)
    sides = members * SPLIT
    pick = ints((sides, wide), 1) == half * ints((sides, wide), 0) + mine // stations
    held[...] = exact_dot_t(pick.astype(jnp.float32), valid)
    pick = ints((members, wide), 1) == stations * ints((members, wide), 0) + lax.rem(mine, stations)
    valid_right = exact_dot_t(pick.astype(jnp.float32), valid)
    owners = owners_ref[...]
    blocks = owners.shape[1]
    earlier = (ints((blocks, blocks), 0) < ints((blocks, blocks), 1)).astype(jnp.float32)
    ontos = []
    for slot in range(CAP):
        named = ints((groups, blocks), 0)
        if slot == 0:
            named = lax.rem(named, outer) * inner + named // outer
        owned = (named == owners).astype(jnp.float32)
        rank = exact_dot(owned, earlier)
        chosen = jnp.where(jnp.abs(rank - slot) < 0.5, owned, 0.0)
        onto = jnp.dot(
            chosen.astype(jnp.bfloat16), spread_ref[...], preferred_element_type=jnp.float32
        )
        ontos.append(onto.astype(jnp.bfloat16))

    load.wait()
    lanes = ints((rows * phases, 128), 1)
    head = raw[:, :, :128].reshape(rows * phases, 128)
    tail = raw[:, :, SEG + taps - 1 - 128 :].reshape(rows * phases, 128)
    tail = pltpu.roll(jnp.where(lanes > 128 - taps, tail, 0.0), 64 + taps - 1, 1)
    ends = jnp.where(lanes < taps - 1, head, tail)
    past = ends * phase_taps[:, 0:1]
    for q in range(1, taps):
        past = past + pltpu.roll(ends, 128 - q, 1) * phase_taps[:, q : q + 1]
    fix = exact_dot(past, edge_ref[...])
    whole[...] = jnp.zeros_like(whole)

    @pl.loop(0, SEG // NB)
    def _(step):
        at = pl.ds(pl.multiple_of(step * NB, NB), NB)
        block = raw[:, :, at].reshape(rows * phases, NB)
        upper = block.astype(jnp.bfloat16)
        lower = (block - upper.astype(jnp.float32)).astype(jnp.bfloat16)
        table = waves[at, :]
        total = jnp.dot(upper, table, preferred_element_type=jnp.float32)
        total = total + jnp.dot(upper, rest[at, :], preferred_element_type=jnp.float32)
        total = total + jnp.dot(lower, table, preferred_element_type=jnp.float32)
        whole[...] += total

    whole_re, whole_im = whole[:, :NB], whole[:, NB:]
    gain_re, gain_im = gains[:, :NB], gains[:, NB:]
    join = (ints((rows, rows * phases), 1) // phases == ints((rows, rows * phases), 0)).astype(jnp.float32)
    real = exact_dot(join, whole_re * gain_re - whole_im * gain_im + fix[:, :NB])
    imag = exact_dot(join, whole_re * gain_im + whole_im * gain_re + fix[:, NB:])
    smoothed = exact_dot(real * real + imag * imag, smooth_ref[...])
    whitener = own / jnp.sqrt(smoothed + EPSILON)
    white[:, :, :NB] = (real * whitener).astype(jnp.bfloat16).reshape(stations, windows, NB)
    white[:, :, NB:] = (imag * whitener).astype(jnp.bfloat16).reshape(stations, windows, NB)

    def near(k):
        peer = lax.rem(mine + k, members)
        side_a, side_c = peer // stations, lax.rem(peer, stations)
        copies = []
        for part in range(SPLIT + 1):
            station = side_c if part == SPLIT else part * half + side_a
            into = right.at[mine] if part == SPLIT else left.at[mine, part]
            copies.append(
                pltpu.make_async_remote_copy(
                    src_ref=white.at[station],
                    dst_ref=into,
                    send_sem=near_send.at[k, part],
                    recv_sem=near_recv.at[k, part],
                    device_id={"sta": peer},
                    device_id_type=pl.DeviceIdType.MESH,
                )
            )
        return copies

    pl.semaphore_wait(barrier, members - 1 + inner - 1 + outer - 1)
    for k in range(1, members):
        for copy in near(k):
            copy.start()
    for part in range(SPLIT):
        left[mine, part] = white[part * half + mine // stations]
    right[mine] = white[lax.rem(mine, stations)]
    for k in range(1, members):
        for copy in near(k):
            copy.wait()

    @pl.loop(0, members * SPLIT, unroll=4)
    def _(n):
        i, h = n // SPLIT, lax.rem(n, SPLIT)
        ours = left[i, h].astype(jnp.float32)
        theirs = right[...].astype(jnp.float32)
        lr, li = ours[None, :, :NB], ours[None, :, NB:]
        rr, ri = theirs[:, :, :NB], theirs[:, :, NB:]
        rows = pl.ds(pl.multiple_of(n * members, members), members)
        count = jnp.sum(held[pl.ds(n, 1), :] * valid_right, axis=1, keepdims=True)
        scale = 1.0 / (math.sqrt(NB) * jnp.maximum(count, 1.0))
        stack[rows, :NB] = jnp.sum(lr * rr + li * ri, axis=1) * scale
        stack[rows, NB:] = jnp.sum(li * rr - lr * ri, axis=1) * scale

    lead_re, lead_im = lead_ref[0:1], lead_ref[1:2]
    stack_re, stack_im = stack[:, :NB], stack[:, NB:]
    moved_re = (stack_re * lead_re - stack_im * lead_im).astype(jnp.bfloat16)
    moved_im = (stack_re * lead_im + stack_im * lead_re).astype(jnp.bfloat16)
    for slot in range(CAP):
        for part, moved in enumerate((moved_re, moved_im)):
            placed = jnp.dot(ontos[slot], moved, preferred_element_type=jnp.float32)
            for chunk in range(NB // 128):
                row = part * (NB // 128) + chunk
                staged[slot, :, row, :] = placed[:, chunk * 128 : (chunk + 1) * 128]
    for slot, side in enumerate((routed_z, routed_y)):
        side[...] = staged[slot].astype(jnp.bfloat16).reshape(side.shape)

    def along_z(k, src, dst, first):
        peer = lax.rem(place + k, inner)
        return pltpu.make_async_remote_copy(
            src_ref=src.at[peer] if first else src.at[:, peer],
            dst_ref=dst.at[place],
            send_sem=far_send.at[1 - first, k],
            recv_sem=far_recv.at[1 - first, k],
            device_id={"grp": line * inner + peer},
            device_id_type=pl.DeviceIdType.MESH,
        )

    def along_y(k, src, dst, first):
        peer = lax.rem(line + k, outer)
        return pltpu.make_async_remote_copy(
            src_ref=src.at[peer] if first else src.at[:, peer],
            dst_ref=dst.at[line],
            send_sem=far_send.at[1 - first, inner + k],
            recv_sem=far_recv.at[1 - first, inner + k],
            device_id={"grp": peer * inner + place},
            device_id_type=pl.DeviceIdType.MESH,
        )

    far_z = sorted(range(1, inner), key=lambda k: -min(k, inner - k))
    far_y = sorted(range(1, outer), key=lambda k: -min(k, outer - k))
    copies = [along_z(k, routed_z, passing_z, 1) for k in far_z]
    copies += [along_y(k, routed_y, passing_y, 1) for k in far_y]
    for copy in copies:
        copy.start()
    passing_z[place] = routed_z[place]
    passing_y[line] = routed_y[line]
    for copy in copies:
        copy.wait()
    copies = [along_y(k, passing_z, arrived_y, 0) for k in far_y]
    copies += [along_z(k, passing_y, arrived_z, 0) for k in far_z]
    for copy in copies:
        copy.start()
    arrived_y[line] = passing_z[:, line]
    arrived_z[place] = passing_y[:, place]
    for copy in copies:
        copy.wait()
    for n in range(outer):
        out_ref[0, n * inner : (n + 1) * inner] = arrived_y[n]
        out_ref[1, n * inner : (n + 1) * inner] = arrived_z[:, n]


def to_lags(arrived_ref, coarse_ref, fine_ref, out_ref, staged):
    staged[...] = arrived_ref[...].astype(jnp.float32)
    chunks = 2 * NB // 128
    sides = []
    for slot in range(CAP):
        parts = [staged[slot, :, c, :] for c in range(chunks)]
        sides.append(jnp.concatenate(parts, axis=1))
    stacks = jnp.concatenate(sides, axis=0).astype(jnp.bfloat16)
    groups = arrived_ref.shape[1]
    fr, fi = fine_ref[:, :NB], fine_ref[:, NB:]
    lags = out_ref.shape[-1]
    wide = 2 * STEP
    for first in range(0, lags, wide):
        real, imag = [], []
        for step in range(first // STEP, (first + wide) // STEP):
            cr, ci = coarse_ref[step : step + 1, :NB], coarse_ref[step : step + 1, NB:]
            real.append((cr * fr - ci * fi).astype(jnp.bfloat16))
            imag.append((cr * fi + ci * fr).astype(jnp.bfloat16))
        table = jnp.concatenate(
            [jnp.concatenate(real, axis=0), jnp.concatenate(imag, axis=0)], axis=1
        )
        block = lax.dot_general(
            stacks, table, (((1,), (1,)), ((), ())), preferred_element_type=jnp.float32
        )
        width = min(wide, lags - first)
        for slot in range(CAP):
            out_ref[:, slot, 0, first : first + width] = block[
                slot * groups : (slot + 1) * groups, :width
            ]


def local(seismograms, fir_taps, valid_windows, pair_owners):
    stations, windows, phases, samples = seismograms.shape
    members = lax.axis_size("sta")
    groups = lax.axis_size("grp")
    taps = fir_taps.shape[1]
    rows = stations * windows
    combos = members * SPLIT * members
    raw = seismograms.reshape(rows, phases, samples)
    coarse, fine = wave_steps()
    adv, edges = edge_waves(taps)
    lead = np.concatenate(turn([MAXLAG]))
    spread = jnp.asarray(pair_spread(members), jnp.bfloat16)

    vmem = pl.BlockSpec(memory_space=pltpu.VMEM)
    tile = (CAP, groups, 2 * NB // 128, 128)
    inner = min(INNER, groups)
    outer = groups // inner
    arrived = pl.pallas_call(
        functools.partial(combine, members, groups, stations, windows, phases),
        out_shape=jax.ShapeDtypeStruct(tile, jnp.bfloat16),
        in_specs=[pl.BlockSpec(memory_space=pl.ANY)] + [vmem] * 10,
        out_specs=vmem,
        scratch_shapes=[
            pltpu.VMEM((rows, phases, samples), jnp.float32),
            pltpu.VMEM((SEG, 2 * NB), jnp.bfloat16),
            pltpu.VMEM((SEG, 2 * NB), jnp.bfloat16),
            pltpu.VMEM((rows * phases, 2 * NB), jnp.float32),
            pltpu.VMEM((stations, windows, 2 * NB), jnp.bfloat16),
            pltpu.VMEM((members, SPLIT, windows, 2 * NB), jnp.bfloat16),
            pltpu.VMEM((members, windows, 2 * NB), jnp.bfloat16),
            pltpu.VMEM((combos, 2 * NB), jnp.float32),
            pltpu.VMEM((members * SPLIT, windows), jnp.float32),
            pltpu.VMEM(tile, jnp.float32),
            pltpu.VMEM((inner, outer) + tile[2:], jnp.bfloat16),
            pltpu.VMEM((inner, outer) + tile[2:], jnp.bfloat16),
            pltpu.VMEM((outer, inner) + tile[2:], jnp.bfloat16),
            pltpu.VMEM((outer, inner) + tile[2:], jnp.bfloat16),
            pltpu.VMEM((outer, inner) + tile[2:], jnp.bfloat16),
            pltpu.VMEM((inner, outer) + tile[2:], jnp.bfloat16),
            pltpu.SemaphoreType.DMA,
            pltpu.SemaphoreType.DMA((members, SPLIT + 1)),
            pltpu.SemaphoreType.DMA((members, SPLIT + 1)),
            pltpu.SemaphoreType.DMA((2, inner + outer)),
            pltpu.SemaphoreType.DMA((2, inner + outer)),
        ],
        compiler_params=pltpu.CompilerParams(collective_id=0, has_side_effects=True),
        name="combine",
    )(
        raw,
        fir_taps,
        valid_windows.T,
        pair_owners.reshape(1, -1),
        coarse,
        fine,
        adv,
        edges,
        smoother(),
        lead,
        spread,
    )
    lagged = pl.pallas_call(
        to_lags,
        out_shape=jax.ShapeDtypeStruct((groups, CAP, 1, 2 * MAXLAG + 1), jnp.float32),
        in_specs=[vmem] * 3,
        out_specs=vmem,
        scratch_shapes=[pltpu.VMEM(tile, jnp.float32)],
        name="to_lags",
    )(arrived, coarse, fine)
    return lagged[None, :, :, :, :]


def solution(mesh):
    in_specs = (P(("grp", "sta"), None, None, None), P(), P("grp", None), P("grp", None, None))
    out_specs = P("grp", None, None, "sta", None)
    return jax.shard_map(local, mesh=mesh, in_specs=in_specs, out_specs=out_specs, check_vma=False)
```
